32 devices in a mesh: groups: 2 (over y), seq: 4 (over x, core), tensor: 4 (over z).
Axes of the slice: x: 2, y: 2, z: 4, core: 2. Of those that a mesh axis runs over, the one named last changes fastest.
Arguments:
- patches: bfloat16 [2056, 1280], P(('groups', 'seq')), parts along dimension 0, may hold values from -6 to 6
- latents: bfloat16 [64, 1280], replicated, may hold values from -160 to 160
- wq_res: bfloat16 [1280, 1536], P(None, 'tensor'), may hold values from -0.15625 to 0.15625
- wk_res: bfloat16 [1280, 1536], P(None, 'tensor'), may hold values from -0.3125 to 0.3125
- wv_res: bfloat16 [1280, 1536], P(None, 'tensor'), may hold values from -0.15625 to 0.15625
- wo_res: bfloat16 [1536, 1280], P('tensor'), may hold values from -0.625 to 0.625
- text: bfloat16 [3072, 8192], P('groups', 'seq'), parts along dimension 0, may hold values from -240 to 240
- norm_gain: bfloat16 [8192], P('seq'), may hold values from 0.25 to 1.75
- wq_x: bfloat16 [8192, 8192], P('seq', 'tensor'), may hold values from -0.0625 to 0.0625
- wk_x: bfloat16 [1280, 8192], P(None, 'tensor'), may hold values from -0.15625 to 0.15625
- wv_x: bfloat16 [1280, 8192], P(None, 'tensor'), may hold values from -0.15625 to 0.15625
- wo_x: bfloat16 [8192, 8192], P('tensor', 'seq'), may hold values from -0.25 to 0.25
- gate_x: float32 [8192], P('seq'), may hold values from -1.5 to 1.5
- text_image: int32 [3072], P('groups'), parts along dimension 0, may hold values from -1 to 3, as said below
Outputs:
- text_out: float32 [3072, 8192], P('groups', 'seq'), parts along dimension 0
- page_latents: bfloat16 [512, 1280], P(('groups', 'seq')), parts along dimension 0
The draws below stay inside these ranges and needn't reach their ends.
There are 2 independent parts, one for each index of `groups`. The reference program is written for one: setup_inputs(seed, part) draws one part's arguments, and reference() takes and returns one part's arrays. A program takes and returns all parts, laid end to end along the dimension named above; an argument that names none is the same for every part. Nothing has to cross between parts.
Inputs may be any that keep to these rules, and one draw needn't show every extreme that they name: text_image[t] is the index of the last image placed at or before token t, -1 before the first image; it never falls along the tokens, and every one of the 4 images is the value of some tokens.
All inputs are finite; a program needn't handle non-finite values.
Results may differ from the reference program's by a relative error of at most 0.015.
The reference program's roundings to bfloat16 on the way count: a program that leaves them out, or rounds other values in their place, can miss the bound.
Values may be sent and summed in bfloat16 or wider, within the bound.
A program may use at most 192 MiB of HBM per device.

```python
import math
import jax
import jax.numpy as jnp
from jax import lax

WIDTH = 8192
HEAD = 128
LATENTS = 64
VIS_WIDTH = 1280
RES_HEADS = 16
RES_HEAD = 96
PATCH_IMG = 257
TEXT = 1536
IMAGES = 4
RES_INNER = 1536
N_TENSOR = 4


def draw_latents(key, part):
    first_key = jax.random.fold_in(key, 0)
    drawn = jnp.clip(jax.random.normal(first_key, (LATENTS, VIS_WIDTH), jnp.float32), -6.0, 6.0)
    return drawn.astype(jnp.bfloat16)


def draw_text(key, part):
    first_key, second_key = jax.random.split(key, 2)
    column = jnp.arange(WIDTH, dtype=jnp.float32) / WIDTH
    ramp = jnp.exp(math.log(3.0) * column)
    rough = jax.random.uniform(second_key, (WIDTH,), jnp.float32, 0.6, 1.5)
    drawn = jnp.clip(jax.random.normal(first_key, (TEXT, WIDTH), jnp.float32), -6.0, 6.0)
    return (drawn * ramp * rough).astype(jnp.bfloat16)


def draw_text_image(key, part):
    lower = max(1, TEXT // (2 * (IMAGES + 1)))
    upper = TEXT // (IMAGES + 1) + 1
    spacing = jax.random.randint(key, (IMAGES,), lower, upper, jnp.int32)
    starts = jnp.cumsum(spacing).astype(jnp.int32)
    positions = jnp.arange(TEXT, dtype=jnp.int32)
    placed = (starts[None, :] <= positions[:, None]).astype(jnp.int32)
    return (jnp.sum(placed, axis=1) - 1).astype(jnp.int32)


def shard_levels(rng, dims, cuts, low, top_value):
    def one(position, blocks):
        heights = jax.random.uniform(jax.random.fold_in(jax.random.fold_in(rng, 6), position), (blocks,), jnp.float32, low / len(cuts), top_value / len(cuts))
        return jnp.repeat(jnp.exp(heights), dims[position] // blocks).reshape((-1,) + (1,) * (len(dims) - position - 1))

    gain = one(*cuts[0])
    for cut in cuts[1:]:
        gain = gain * one(*cut)
    return gain


def bell_draw(rng, dims, deviation, most, cuts=(), kind=jnp.bfloat16):
    values = deviation * jax.random.normal(rng, dims, jnp.float32)
    if cuts:
        values = values * shard_levels(rng, dims, cuts, -0.22, 0.18)
    return jnp.clip(values, -most, most).astype(kind)


def setup_inputs(seed: int = 0, part: int = 0) -> dict:
    keys = jax.random.split(jax.random.key(seed), 15)
    own_keys = jax.random.split(jax.random.fold_in(keys[14], part), 15)
    patches = bell_draw(own_keys[0], (IMAGES * PATCH_IMG, VIS_WIDTH), 1.0, 6.0, ((0, 4),))
    latents = draw_latents(jax.random.fold_in(keys[14], 71), part)
    wq_res = bell_draw(keys[2], (VIS_WIDTH, RES_INNER), VIS_WIDTH ** -0.5, 0.15625, ((1, 4),))
    wk_res = bell_draw(keys[3], (VIS_WIDTH, RES_INNER), (VIS_WIDTH // 4) ** -0.5, 0.3125, ((1, 4),))
    wv_res = bell_draw(keys[4], (VIS_WIDTH, RES_INNER), VIS_WIDTH ** -0.5, 0.15625, ((1, 4),))
    wo_res = bell_draw(keys[5], (RES_INNER, VIS_WIDTH), RES_HEAD ** -0.5, 0.625, ((0, 4),))
    text = draw_text(jax.random.fold_in(jax.random.fold_in(keys[14], part), 71), part)
    norm_gain = jnp.clip(1.0 + 0.15 * jax.random.normal(keys[7], (WIDTH,), jnp.float32), 0.25, 1.75).astype(jnp.bfloat16)
    wq_x = bell_draw(keys[8], (WIDTH, WIDTH), WIDTH ** -0.5, 0.0625, ((0, 4), (1, 4)))
    wk_x = bell_draw(keys[9], (VIS_WIDTH, WIDTH), VIS_WIDTH ** -0.5, 0.15625, ((1, 4),))
    wv_x = bell_draw(keys[10], (VIS_WIDTH, WIDTH), VIS_WIDTH ** -0.5, 0.15625, ((1, 4),))
    wo_x = bell_draw(keys[11], (WIDTH, WIDTH), (WIDTH // 16) ** -0.5, 0.25, ((0, 4), (1, 4)))
    gate_x = jnp.clip(jax.random.uniform(keys[12], (WIDTH,), jnp.float32, -1.5, 1.5) * shard_levels(keys[12], (WIDTH,), ((0, 4),), -0.4, 0.0), -1.5, 1.5)
    text_image = draw_text_image(jax.random.fold_in(jax.random.fold_in(keys[14], part), 71), part)
    return dict(patches=patches, latents=latents, wq_res=wq_res, wk_res=wk_res, wv_res=wv_res, wo_res=wo_res, text=text, norm_gain=norm_gain, wq_x=wq_x, wk_x=wk_x, wv_x=wv_x, wo_x=wo_x, gate_x=gate_x, text_image=text_image)


def reference(patches, latents, wq_res, wk_res, wv_res, wo_res, text, norm_gain, wq_x, wk_x, wv_x, wo_x, gate_x, text_image):
    inv_res = 1.0 / math.sqrt(RES_HEAD)
    inv_root = 1.0 / math.sqrt(HEAD)
    queries = jnp.dot(latents, wq_res, preferred_element_type=jnp.float32).astype(jnp.bfloat16).reshape(LATENTS, RES_HEADS, RES_HEAD)
    page_keys = jnp.dot(patches, wk_res, preferred_element_type=jnp.float32).astype(jnp.bfloat16).reshape(IMAGES, PATCH_IMG, RES_HEADS, RES_HEAD)
    page_values = jnp.dot(patches, wv_res, preferred_element_type=jnp.float32).astype(jnp.bfloat16).reshape(IMAGES, PATCH_IMG, RES_HEADS, RES_HEAD)
    scores = jnp.einsum('lhd,iphd->ihlp', queries.astype(jnp.float32), page_keys.astype(jnp.float32)) * inv_res
    summit = lax.optimization_barrier(jnp.max(scores, axis=3, keepdims=True))
    rounded = jnp.exp(scores - summit).astype(jnp.bfloat16)
    weights = lax.optimization_barrier(rounded).astype(jnp.float32)
    totals = lax.optimization_barrier(jnp.sum(weights, axis=3))
    blended = jnp.einsum('ihlp,iphd->ihld', weights, page_values.astype(jnp.float32))
    pooled = (blended / totals[:, :, :, None]).transpose(0, 2, 1, 3).reshape(IMAGES * LATENTS, RES_INNER).astype(jnp.bfloat16)
    repeated = jnp.tile(latents.astype(jnp.float32), (IMAGES, 1))
    page_latents = (repeated + jnp.dot(pooled, wo_res, preferred_element_type=jnp.float32)).astype(jnp.bfloat16)
    hidden = text.astype(jnp.float32)
    inverse = lax.rsqrt(lax.optimization_barrier(jnp.mean(hidden * hidden, axis=1)) + 1e-05)
    scaled = (hidden * norm_gain.astype(jnp.float32)).astype(jnp.bfloat16)
    heads_x = WIDTH // HEAD
    text_queries = (jnp.dot(scaled, wq_x, preferred_element_type=jnp.float32) * inverse[:, None]).astype(jnp.bfloat16).reshape(TEXT, heads_x, HEAD)
    cross_keys = jnp.dot(page_latents, wk_x, preferred_element_type=jnp.float32).astype(jnp.bfloat16).reshape(IMAGES * LATENTS, heads_x, HEAD)
    cross_values = jnp.dot(page_latents, wv_x, preferred_element_type=jnp.float32).astype(jnp.bfloat16).reshape(IMAGES * LATENTS, heads_x, HEAD)
    latent_owner = jnp.arange(IMAGES * LATENTS, dtype=jnp.int32) // LATENTS
    allowed = text_image[:, None] == latent_owner[None, :]

    def one_head(operands):
        head_q, head_k, head_v = operands
        logits = jnp.dot(head_q.astype(jnp.float32), head_k.astype(jnp.float32).T) * inv_root
        logits = jnp.where(allowed, logits, -1e+30)
        row_peak = lax.optimization_barrier(jnp.max(logits, axis=1, keepdims=True))
        head_round = jnp.exp(logits - row_peak).astype(jnp.bfloat16)
        head_weights = lax.optimization_barrier(head_round).astype(jnp.float32)
        row_total = lax.optimization_barrier(jnp.sum(head_weights, axis=1))
        mixture = jnp.dot(head_weights, head_v.astype(jnp.float32))
        return mixture / row_total[:, None]
    per_head = lax.map(one_head, (text_queries.transpose(1, 0, 2), cross_keys.transpose(1, 0, 2), cross_values.transpose(1, 0, 2)))
    visible = (text_image >= 0).astype(jnp.float32)
    attended = (per_head.transpose(1, 0, 2) * visible[:, None, None]).astype(jnp.bfloat16).reshape(TEXT, WIDTH)
    col_group = WIDTH // N_TENSOR
    att_groups = attended.reshape(TEXT, N_TENSOR, col_group).transpose(1, 0, 2)
    wo_groups = wo_x.reshape(N_TENSOR, col_group, WIDTH)

    def add_group(running, inputs):
        term = lax.optimization_barrier(jnp.dot(inputs[0], inputs[1], preferred_element_type=jnp.float32).astype(jnp.bfloat16)).astype(jnp.float32)
        return (running + term, None)
    branch, unused = lax.scan(add_group, jnp.zeros((TEXT, WIDTH), jnp.float32), (att_groups, wo_groups))
    text_out = hidden + jnp.tanh(gate_x.astype(jnp.float32)) * branch
    return (text_out, page_latents)
```

```python
import functools
import math

import jax
import jax.numpy as jnp
from jax import lax
from jax.experimental import pallas as pl
from jax.experimental.pallas import tpu as pltpu
from jax.sharding import PartitionSpec as P

WIDTH = 8192
HEAD = 128
RES_HEAD = 96
PATCH_IMG = 257
CHUNKS = 4
BF = jnp.bfloat16
F32 = jnp.float32


def shifted(value, axis, count, step):
    pairs = [(i, (i + step) % count) for i in range(count)]
    return lax.ppermute(value, axis, pairs)


def attend_kernel(heads, q_ref, k_ref, v_ref, img_ref, own_ref, o_ref):
    img = img_ref[...]
    allowed = img == own_ref[...]
    visible = (img >= 0).astype(F32)
    scale = 1.0 / math.sqrt(HEAD)
    for h in range(heads):
        cols = slice(h * HEAD, (h + 1) * HEAD)
        logits = lax.dot_general(
            q_ref[:, cols], k_ref[:, cols], (((1,), (1,)), ((), ())), preferred_element_type=F32
        )
        logits = jnp.where(allowed, logits * scale, -1e30)
        peak = jnp.max(logits, axis=1, keepdims=True)
        probs = jnp.exp(logits - peak).astype(BF)
        total = jnp.sum(probs.astype(F32), axis=1, keepdims=True)
        mixed = jnp.dot(probs, v_ref[:, cols], preferred_element_type=F32)
        o_ref[:, cols] = (mixed / total * visible).astype(BF)


def attend(q, keys, values, img, owner):
    rows, cols = q.shape
    heads = cols // HEAD
    lat = keys.shape[0]
    return pl.pallas_call(
        functools.partial(attend_kernel, heads),
        out_shape=jax.ShapeDtypeStruct((rows, cols), BF),
        in_specs=[pl.BlockSpec(memory_space=pltpu.VMEM)] * 5,
        out_specs=pl.BlockSpec(memory_space=pltpu.VMEM),
        cost_estimate=pl.CostEstimate(
            flops=4 * rows * lat * cols,
            bytes_accessed=4 * (rows + lat) * cols,
            transcendentals=rows * lat * heads,
        ),
        name="attend",
    )(q, keys, values, img, owner)


def resample(patches, latents, wq_res, wk_res, wv_res, wo_res):
    inv_res = 1.0 / math.sqrt(RES_HEAD)
    lat_count = latents.shape[0]
    img_count = patches.shape[0] // PATCH_IMG
    heads_res = wq_res.shape[1] // RES_HEAD
    queries = (
        jnp.dot(latents, wq_res, preferred_element_type=F32)
        .astype(BF)
        .reshape(lat_count, heads_res, RES_HEAD)
    )
    page_keys = (
        jnp.dot(patches, wk_res, preferred_element_type=F32)
        .astype(BF)
        .reshape(img_count, PATCH_IMG, heads_res, RES_HEAD)
    )
    page_values = (
        jnp.dot(patches, wv_res, preferred_element_type=F32)
        .astype(BF)
        .reshape(img_count, PATCH_IMG, heads_res, RES_HEAD)
    )
    scores = jnp.einsum("lhd,iphd->ihlp", queries, page_keys, preferred_element_type=F32) * inv_res
    summit = jnp.max(scores, axis=3, keepdims=True)
    weights = jnp.exp(scores - summit).astype(BF)
    totals = jnp.sum(weights, axis=3, dtype=F32)
    blended = jnp.einsum("ihlp,iphd->ihld", weights, page_values, preferred_element_type=F32)
    pooled = (
        (blended / totals[:, :, :, None])
        .transpose(0, 2, 1, 3)
        .reshape(img_count * lat_count, heads_res * RES_HEAD)
        .astype(BF)
    )
    return jnp.dot(pooled, wo_res, preferred_element_type=F32)


def take(value, index, axis=0):
    return lax.dynamic_index_in_dim(value, index, axis, keepdims=False)


def ahead(index, step, count):
    return lax.rem(index + jnp.uint32(step), jnp.uint32(count))


def cyclic_order(pieces, me, count):
    out = jnp.zeros((count,) + pieces[0].shape, pieces[0].dtype)
    for k, piece in enumerate(pieces):
        at = ahead(me, count - k, count)
        out = lax.dynamic_update_index_in_dim(out, piece, at, 0)
    return out


def make_shards(n_seq, n_tensor):
    n_x = n_seq // 2
    core_pairs = [(i, i ^ 1) for i in range(n_seq)]

    def x_shift(value, step):
        pairs = [(i, (i + 2 * step) % n_seq) for i in range(n_seq)]
        return lax.ppermute(value, "seq", pairs)

    def shards(
        patches,
        latents,
        wq_res,
        wk_res,
        wv_res,
        wo_res,
        text,
        norm_gain,
        wq_x,
        wk_x,
        wv_x,
        wo_x,
        gate_x,
        text_image,
    ):
        seq_me = lax.axis_index("seq").astype(jnp.uint32)
        ten_me = lax.axis_index("tensor").astype(jnp.uint32)
        core, x_me = seq_me & 1, seq_me >> 1
        lat_count = latents.shape[0]
        img_count = patches.shape[0] // PATCH_IMG
        tok_count, feat = text.shape
        width = wq_x.shape[1]
        sub = tok_count // (CHUNKS * n_seq)

        partial_value = resample(patches, latents, wq_res, wk_res, wv_res, wo_res)
        lat_rows = partial_value.shape[0]
        part_rows = lat_rows // n_tensor
        by_owner = partial_value.reshape(n_tensor, part_rows, -1)

        def owner_part(index):
            return take(by_owner, index)

        latent_sum = owner_part(ten_me)
        for k in range(1, n_tensor):
            latent_sum = latent_sum + shifted(
                owner_part(ahead(ten_me, k, n_tensor)), "tensor", n_tensor, k
            )
        repeated = jnp.tile(latents, (img_count, 1)).reshape(n_tensor, part_rows, -1)
        own_lat = take(repeated, ten_me)
        own_page = (own_lat.astype(F32) + latent_sum).astype(BF)
        page_parts = [own_page] + [
            shifted(own_page, "tensor", n_tensor, k) for k in range(1, n_tensor)
        ]
        page_latents = cyclic_order(page_parts, ten_me, n_tensor).reshape(lat_rows, -1)

        hidden = text.astype(F32)
        squares = jnp.sum(hidden * hidden, axis=1)
        square_sum = squares
        for k in range(1, n_seq):
            square_sum = square_sum + shifted(squares, "seq", n_seq, k)
        inverse = lax.rsqrt(square_sum / WIDTH + 1e-05)
        blocks = text.reshape(CHUNKS, 2, n_x * sub, feat)

        def core_queries(which):
            rows = take(blocks, which, 1)
            scaled = (rows.astype(F32) * norm_gain.astype(F32)).astype(BF)
            return jnp.dot(
                scaled.reshape(-1, feat), wq_x, preferred_element_type=F32
            ).reshape(CHUNKS, n_x, sub, width)

        away = core_queries(1 - core).astype(BF)
        from_core = lax.ppermute(away, "seq", core_pairs)
        half_sum = core_queries(core) + from_core.astype(F32)

        inv_blocks = inverse.reshape(CHUNKS, n_seq, sub)
        img_blocks = text_image.reshape(CHUNKS, n_seq, sub)
        my_block = core * n_x + x_me

        queries = []
        for c in range(CHUNKS):
            total = take(half_sum[c], x_me)
            for k in range(1, n_x):
                there = take(half_sum[c], ahead(x_me, k, n_x))
                total = total + x_shift(there.astype(BF), k).astype(F32)
            inv = take(inv_blocks[c], my_block)
            queries.append((total * inv[:, None]).astype(BF))

        page_all = [page_latents] + [
            shifted(page_latents, "seq", n_seq, k) for k in range(1, n_seq)
        ]
        page_all = jnp.concatenate(page_all, axis=0)
        keys = jnp.dot(page_all, wk_x, preferred_element_type=F32).astype(BF)
        values = jnp.dot(page_all, wv_x, preferred_element_type=F32).astype(BF)
        holder = jnp.concatenate(
            [
                ahead(seq_me, n_seq - k, n_seq).astype(jnp.int32) * img_count
                + jnp.arange(lat_rows, dtype=jnp.int32) // lat_count
                for k in range(n_seq)
            ]
        )[None, :]

        gate_open = jnp.tanh(gate_x)
        def finish(out, branch, c):
            for j in range(n_seq):
                side, k = (core if j < n_x else 1 - core), j % n_x
                start = (c * n_seq + side * n_x + ahead(x_me, n_x - k, n_x)) * sub
                piece = branch[j * sub : (j + 1) * sub].astype(F32)
                old = lax.dynamic_slice_in_dim(text, start, sub, 0).astype(F32)
                out = lax.dynamic_update_slice_in_dim(out, old + gate_open * piece, start, 0)
            return out

        text_out = jnp.zeros((tok_count, feat), F32)
        previous = None
        for c in range(CHUNKS):
            img = take(img_blocks[c], my_block)
            own = attend(queries[c], keys, values, img[:, None], holder)
            along_x = [own] + [x_shift(own, k) for k in range(1, n_x)]
            mine = jnp.concatenate(along_x, axis=0)
            other = lax.ppermute(mine, "seq", core_pairs)
            rows = jnp.concatenate([mine, other], axis=0)
            block_part = jnp.dot(rows, wo_x, preferred_element_type=F32)
            part = block_part.astype(BF)
            if c:
                part, previous = lax.optimization_barrier((part, previous))
                text_out = finish(text_out, previous, c - 1)
            previous = lax.psum(part, "tensor")
        text_out = finish(text_out, previous, CHUNKS - 1)
        return (text_out, page_latents)
    return shards


def solution(mesh):
    in_specs = (
        P(("groups", "seq"), None),
        P(),
        P(None, "tensor"),
        P(None, "tensor"),
        P(None, "tensor"),
        P("tensor", None),
        P("groups", "seq"),
        P("seq"),
        P("seq", "tensor"),
        P(None, "tensor"),
        P(None, "tensor"),
        P("tensor", "seq"),
        P("seq"),
        P("groups"),
    )
    out_specs = (P("groups", "seq"), P(("groups", "seq"), None))
    shards = make_shards(mesh.shape["seq"], mesh.shape["tensor"])
    return jax.shard_map(shards, mesh=mesh, in_specs=in_specs, out_specs=out_specs, check_vma=False)
```

```python
import functools
import math

import jax
import jax.numpy as jnp
from jax import lax
from jax.experimental import pallas as pl
from jax.experimental.pallas import tpu as pltpu
from jax.sharding import PartitionSpec as P

WIDTH = 8192
HEAD = 128
RES_HEAD = 96
PATCH_IMG = 257
CHUNKS = 2
BF = jnp.bfloat16
F32 = jnp.float32


def shifted(value, axis, count, step):
    pairs = [(i, (i + step) % count) for i in range(count)]
    return lax.ppermute(value, axis, pairs)


def attend_kernel(heads, q_ref, k_ref, v_ref, img_ref, own_ref, o_ref):
    img = img_ref[...]
    allowed = img == own_ref[...]
    visible = (img >= 0).astype(F32)
    scale = 1.0 / math.sqrt(HEAD)
    for h in range(heads):
        cols = slice(h * HEAD, (h + 1) * HEAD)
        logits = lax.dot_general(
            q_ref[:, cols], k_ref[:, cols], (((1,), (1,)), ((), ())), preferred_element_type=F32
        )
        logits = jnp.where(allowed, logits * scale, -1e30)
        peak = jnp.max(logits, axis=1, keepdims=True)
        probs = jnp.exp(logits - peak).astype(BF)
        total = jnp.sum(probs.astype(F32), axis=1, keepdims=True)
        mixed = jnp.dot(probs, v_ref[:, cols], preferred_element_type=F32)
        o_ref[:, cols] = (mixed / total * visible).astype(BF)


def attend(q, keys, values, img, owner):
    rows, cols = q.shape
    heads = cols // HEAD
    lat = keys.shape[0]
    return pl.pallas_call(
        functools.partial(attend_kernel, heads),
        out_shape=jax.ShapeDtypeStruct((rows, cols), BF),
        in_specs=[pl.BlockSpec(memory_space=pltpu.VMEM)] * 5,
        out_specs=pl.BlockSpec(memory_space=pltpu.VMEM),
        cost_estimate=pl.CostEstimate(
            flops=4 * rows * lat * cols,
            bytes_accessed=4 * (rows + lat) * cols,
            transcendentals=rows * lat * heads,
        ),
        name="attend",
    )(q, keys, values, img, owner)


def resample(patches, latents, wq_res, wk_res, wv_res, wo_res):
    inv_res = 1.0 / math.sqrt(RES_HEAD)
    lat_count = latents.shape[0]
    img_count = patches.shape[0] // PATCH_IMG
    heads_res = wq_res.shape[1] // RES_HEAD
    queries = (
        jnp.dot(latents, wq_res, preferred_element_type=F32)
        .astype(BF)
        .reshape(lat_count, heads_res, RES_HEAD)
    )
    page_keys = (
        jnp.dot(patches, wk_res, preferred_element_type=F32)
        .astype(BF)
        .reshape(img_count, PATCH_IMG, heads_res, RES_HEAD)
    )
    page_values = (
        jnp.dot(patches, wv_res, preferred_element_type=F32)
        .astype(BF)
        .reshape(img_count, PATCH_IMG, heads_res, RES_HEAD)
    )
    scores = jnp.einsum("lhd,iphd->ihlp", queries, page_keys, preferred_element_type=F32) * inv_res
    summit = jnp.max(scores, axis=3, keepdims=True)
    weights = jnp.exp(scores - summit).astype(BF)
    totals = jnp.sum(weights, axis=3, dtype=F32)
    blended = jnp.einsum("ihlp,iphd->ihld", weights, page_values, preferred_element_type=F32)
    pooled = (
        (blended / totals[:, :, :, None])
        .transpose(0, 2, 1, 3)
        .reshape(img_count * lat_count, heads_res * RES_HEAD)
        .astype(BF)
    )
    return jnp.dot(pooled, wo_res, preferred_element_type=F32)


def take(value, index, axis=0):
    return lax.dynamic_index_in_dim(value, index, axis, keepdims=False)


def ahead(index, step, count):
    return lax.rem(index + jnp.uint32(step), jnp.uint32(count))


def cyclic_order(pieces, me, count):
    out = jnp.zeros((count,) + pieces[0].shape, pieces[0].dtype)
    for k, piece in enumerate(pieces):
        at = ahead(me, count - k, count)
        out = lax.dynamic_update_index_in_dim(out, piece, at, 0)
    return out


def line_sum_kernel(n, pairs, seg, rows_ref, w_ref, out_ref, part, right, left,
                    send_sem, right_sem, left_sem, back_sem):
    me = lax.axis_index("tensor")
    width = w_ref.shape[1]
    tile = math.gcd(width, 512)

    def product(c):
        @pl.loop(0, width // tile)
        def _(t):
            cols = pl.ds(pl.multiple_of(t * tile, tile), tile)
            value = jnp.dot(rows_ref[c], w_ref[:, cols], preferred_element_type=F32).astype(BF)
            for j in range(n):
                part[c, j, :, cols] = value[j * seg : (j + 1) * seg]

    def add(c, j, came):
        total = part[c, j].astype(F32) + came[c, j].astype(F32)
        part[c, j] = total.astype(BF)

    def copy(src, dst, slot, way, turn, sem):
        return pltpu.make_async_remote_copy(
            src_ref=src,
            dst_ref=dst,
            send_sem=send_sem.at[slot - 1, way, turn],
            recv_sem=sem,
            device_id={"tensor": me + 1 if way == 0 else me - 1},
            device_id_type=pl.DeviceIdType.MESH,
        )

    def place(way):
        return me if way == 0 else n - 1 - me

    def segment(way, j):
        return j if way == 0 else n - 1 - j

    def inward(slot, way, turn, m):
        c, i = 2 * m + turn, place(way)
        came, sem = (right, right_sem) if way == 0 else (left, left_sem)
        j = segment(way, jnp.minimum(n - slot + i, n - 1))
        return i <= slot - 1, c, j, copy(part.at[c, j], came.at[c, j], slot, way, turn, sem.at[c, j])

    def outward(slot, way, turn, m):
        c, i = 2 * (m - 1) + turn, place(way)
        j = segment(way, jnp.maximum(i - slot, 0))
        active = jnp.logical_and(i >= slot, i <= n - 2)
        return active, c, j, copy(out_ref.at[c, j], out_ref.at[c, j], slot, way, turn, back_sem.at[c, j])

    def first(way, turn, m):
        c = 2 * m + turn
        return place(way) <= n - 2, copy(
            out_ref.at[c, me], out_ref.at[c, me], n, way, turn, back_sem.at[c, me]
        )

    def settle(slot, way, turn, m):
        if slot == n:
            go, sent = first(way, turn, m)

            @pl.when(jnp.logical_and(go, jnp.logical_and(m >= 0, m < pairs)))
            def _():
                sent.wait_send()

            return
        go, _, _, sent = inward(slot, way, turn, m)

        @pl.when(jnp.logical_and(go, jnp.logical_and(m >= 0, m < pairs)))
        def _():
            sent.wait_send()

        if slot <= n - 2:
            go, _, _, passed = outward(slot, way, turn, m)

            @pl.when(jnp.logical_and(go, m >= 1))
            def _():
                passed.wait_send()

    barrier = pltpu.get_barrier_semaphore()
    for way in (0, 1):
        @pl.when(place(way) <= n - 2)
        def _(way=way):
            pl.semaphore_signal(
                barrier,
                inc=1,
                device_id={"tensor": me + 1 if way == 0 else me - 1},
                device_id_type=pl.DeviceIdType.MESH,
            )
    product(0)
    pl.semaphore_wait(barrier, jnp.minimum(me, 1) + jnp.minimum(n - 1 - me, 1))
    product(1)

    def iteration(m, carry):
        for slot in range(1, n):
            for turn in (0, 1):
                for way in (0, 1):
                    settle(slot, way, turn, m - 1)
                    go, c, j, out = inward(slot, way, turn, m)

                    @pl.when(jnp.logical_and(go, m < pairs))
                    def _(way=way, c=c, j=j, out=out):
                        @pl.when(place(way) > 0)
                        def _():
                            out.wait_recv()
                            add(c, j, right if way == 0 else left)

                        out.start()

                    if slot <= n - 2:
                        go, c, j, passed = outward(slot, way, turn, m)

                        @pl.when(jnp.logical_and(go, m >= 1))
                        def _(passed=passed):
                            passed.wait_recv()
                            passed.start()

                if turn == 0 and slot in (min(2, n - 1), min(3, n - 1)):
                    for which in (0, 1):
                        if slot == min(2 + which, n - 1):
                            @pl.when(m + 1 < pairs)
                            def _(which=which):
                                product(2 * (m + 1) + which)

        for turn in (0, 1):
            c = 2 * m + turn
            for way in (0, 1):
                settle(n, way, turn, m - 1)

            @pl.when(m < pairs)
            def _(turn=turn, c=c):
                for way in (0, 1):
                    came, sem = (right, right_sem) if way == 0 else (left, left_sem)

                    @pl.when(place(way) > 0)
                    def _(way=way, came=came, sem=sem):
                        copy(part.at[c, me], came.at[c, me], 1, way, turn, sem.at[c, me]).wait_recv()
                        add(c, me, came)

                out_ref[c, me] = part[c, me]
                for way in (0, 1):
                    go, out = first(way, turn, m)

                    @pl.when(go)
                    def _(out=out):
                        out.start()

        return carry

    lax.fori_loop(0, pairs + 1, iteration, 0)
    for turn in (0, 1):
        for way in (0, 1):
            for slot in range(1, n - 1):
                settle(slot, way, turn, pairs)

    for way in (0, 1):
        @pl.when(place(way) == n - 1)
        def _(way=way):
            @pl.loop(0, 2 * pairs)
            def _(c):
                for k in range(n - 1):
                    j = segment(way, k)
                    copy(
                        out_ref.at[c, j], out_ref.at[c, j], 1, way, 0, back_sem.at[c, j]
                    ).wait_recv()


def line_sum(rows, w, n, call):
    count, depth = rows.shape
    width = w.shape[1]
    pairs = max(m for m in (1, 2, 3, 4) if count % (2 * m * n * 16) == 0 or m == 1)
    seg = count // (2 * pairs * n)
    shape = (2 * pairs, n, seg, width)
    out = pl.pallas_call(
        functools.partial(line_sum_kernel, n, pairs, seg),
        out_shape=jax.ShapeDtypeStruct(shape, BF),
        in_specs=[pl.BlockSpec(memory_space=pltpu.VMEM)] * 2,
        out_specs=pl.BlockSpec(memory_space=pltpu.VMEM),
        scratch_shapes=[pltpu.VMEM(shape, BF)] * 3
        + [
            pltpu.SemaphoreType.DMA((n, 2, 2)),
            pltpu.SemaphoreType.DMA((2 * pairs, n)),
            pltpu.SemaphoreType.DMA((2 * pairs, n)),
            pltpu.SemaphoreType.DMA((2 * pairs, n)),
        ],
        compiler_params=pltpu.CompilerParams(
            collective_id=call, has_side_effects=True, vmem_limit_bytes=44 << 20
        ),
        cost_estimate=pl.CostEstimate(
            flops=60 * 2 * count * depth * width, bytes_accessed=0, transcendentals=0
        ),
        name=f"line_sum_{call}",
    )(rows.reshape(2 * pairs, n * seg, depth), w)
    return out.reshape(count, width)


def make_shards(n_seq, n_tensor):
    n_x = n_seq // 2
    core_pairs = [(i, i ^ 1) for i in range(n_seq)]

    def x_shift(value, step):
        pairs = [(i, (i + 2 * step) % n_seq) for i in range(n_seq)]
        return lax.ppermute(value, "seq", pairs)

    def shards(
        patches,
        latents,
        wq_res,
        wk_res,
        wv_res,
        wo_res,
        text,
        norm_gain,
        wq_x,
        wk_x,
        wv_x,
        wo_x,
        gate_x,
        text_image,
    ):
        seq_me = lax.axis_index("seq").astype(jnp.uint32)
        ten_me = lax.axis_index("tensor").astype(jnp.uint32)
        core, x_me = seq_me & 1, seq_me >> 1
        lat_count = latents.shape[0]
        img_count = patches.shape[0] // PATCH_IMG
        tok_count, feat = text.shape
        width = wq_x.shape[1]
        sub = tok_count // (CHUNKS * n_seq)

        partial_value = resample(patches, latents, wq_res, wk_res, wv_res, wo_res)
        lat_rows = partial_value.shape[0]
        part_rows = lat_rows // n_tensor
        by_owner = partial_value.reshape(n_tensor, part_rows, -1)

        def owner_part(index):
            return take(by_owner, index)

        latent_sum = owner_part(ten_me)
        for k in range(1, n_tensor):
            latent_sum = latent_sum + shifted(
                owner_part(ahead(ten_me, k, n_tensor)), "tensor", n_tensor, k
            )
        repeated = jnp.tile(latents, (img_count, 1)).reshape(n_tensor, part_rows, -1)
        own_lat = take(repeated, ten_me)
        own_page = (own_lat.astype(F32) + latent_sum).astype(BF)
        page_parts = [own_page] + [
            shifted(own_page, "tensor", n_tensor, k) for k in range(1, n_tensor)
        ]
        page_latents = cyclic_order(page_parts, ten_me, n_tensor).reshape(lat_rows, -1)

        hidden = text.astype(F32)
        squares = jnp.sum(hidden * hidden, axis=1)
        square_sum = squares
        for k in range(1, n_seq):
            square_sum = square_sum + shifted(squares, "seq", n_seq, k)
        inverse = lax.rsqrt(square_sum / WIDTH + 1e-05)
        blocks = text.reshape(CHUNKS, 2, n_x * sub, feat)

        def core_queries(which):
            rows = take(blocks, which, 1)
            scaled = (rows.astype(F32) * norm_gain.astype(F32)).astype(BF)
            return jnp.dot(
                scaled.reshape(-1, feat), wq_x, preferred_element_type=F32
            ).reshape(CHUNKS, n_x, sub, width)

        away = core_queries(1 - core).astype(BF)
        from_core = lax.ppermute(away, "seq", core_pairs)
        half_sum = core_queries(core) + from_core.astype(F32)

        inv_blocks = inverse.reshape(CHUNKS, n_seq, sub)
        img_blocks = text_image.reshape(CHUNKS, n_seq, sub)
        my_block = core * n_x + x_me

        queries = []
        for c in range(CHUNKS):
            total = take(half_sum[c], x_me)
            for k in range(1, n_x):
                there = take(half_sum[c], ahead(x_me, k, n_x))
                total = total + x_shift(there.astype(BF), k).astype(F32)
            inv = take(inv_blocks[c], my_block)
            queries.append((total * inv[:, None]).astype(BF))

        page_all = [page_latents] + [
            shifted(page_latents, "seq", n_seq, k) for k in range(1, n_seq)
        ]
        page_all = jnp.concatenate(page_all, axis=0)
        keys = jnp.dot(page_all, wk_x, preferred_element_type=F32).astype(BF)
        values = jnp.dot(page_all, wv_x, preferred_element_type=F32).astype(BF)
        holder = jnp.concatenate(
            [
                ahead(seq_me, n_seq - k, n_seq).astype(jnp.int32) * img_count
                + jnp.arange(lat_rows, dtype=jnp.int32) // lat_count
                for k in range(n_seq)
            ]
        )[None, :]

        gate_open = jnp.tanh(gate_x)
        attended = []
        for c in range(CHUNKS):
            img = take(img_blocks[c], my_block)
            own = attend(queries[c], keys, values, img[:, None], holder)
            along_x = [own] + [x_shift(own, k) for k in range(1, n_x)]
            mine = cyclic_order(along_x, x_me, n_x)
            other = lax.ppermute(mine, "seq", core_pairs)
            low = jnp.where(core == 0, mine, other)
            high = jnp.where(core == 0, other, mine)
            attended.append(jnp.concatenate([low, high], axis=0).reshape(n_seq * sub, width))
        branch = [line_sum(part, wo_x, n_tensor, c) for c, part in enumerate(attended)]
        branch = jnp.concatenate(branch, axis=0).astype(F32)
        return (hidden + gate_open * branch, page_latents)

    return shards


def solution(mesh):
    in_specs = (
        P(("groups", "seq"), None),
        P(),
        P(None, "tensor"),
        P(None, "tensor"),
        P(None, "tensor"),
        P("tensor", None),
        P("groups", "seq"),
        P("seq"),
        P("seq", "tensor"),
        P(None, "tensor"),
        P(None, "tensor"),
        P("tensor", "seq"),
        P("seq"),
        P("groups"),
    )
    out_specs = (P("groups", "seq"), P(("groups", "seq"), None))
    shards = make_shards(mesh.shape["seq"], mesh.shape["tensor"])
    return jax.shard_map(shards, mesh=mesh, in_specs=in_specs, out_specs=out_specs, check_vma=False)
```
